1024 devices in a mesh: tpair: 128 (over z, x, core), col: 8 (over y).
Axes of the slice: x: 8, y: 8, z: 8, core: 2. Of those that a mesh axis runs over, the one named last changes fastest.
Arguments:
- peramb: bfloat16 [128, 2, 2048, 2048], P('tpair', None, None, 'col'), may hold values from -6 to 6
- sink_ops: bfloat16 [128, 2, 2, 512, 512], P('tpair'), may hold values from -0.1875 to 0.1875
- op_table: bfloat16 [2048, 2, 512], P('tpair'), may hold values from -0.1875 to 0.1875
- row_slot: int32 [2048], replicated, may hold values from 0 to 2047, each once
- pair_source: int32 [128], P('tpair'), may hold values from 0 to 1
- op_index: int32 [256, 2], P('tpair'), may hold values from 0 to 1
- listed_rows: int32 [256, 128], P('tpair'), may hold values from 0 to 511
Outputs:
- contracted: bfloat16 [256, 4, 128, 2, 2048], P('tpair', None, 'col')
The draws below stay inside these ranges and needn't reach their ends.
Inputs may be any that keep to these rules, and one draw needn't show every extreme that they name: `row_slot`: every position of 0 to 2047 appears once.
All inputs are finite; a program needn't handle non-finite values.
Results may differ from the reference program's by a relative error of at most 0.0049.
Values may be sent and summed in bfloat16 or wider, within the bound.
A program may use at most 64 MiB of HBM per device.

```python
import jax
import jax.numpy as jnp
from jax import lax

NV = 512
NS = 4
ORDER = 2048
NOPS = 2
NSRC = 2
ROWS = 2048
SEL = 128
PROD_DEV = 2
PAIRS = 128
PROD_ALL = 256


def with_ends(entries, rng, low, top_value):
    extent = entries.shape
    place = [jax.random.randint(jax.random.fold_in(rng, axis), (), 0, extent[axis]) for axis in range(len(extent))]
    entries = entries.at[tuple(place)].set(low)
    longest = extent.index(max(extent))
    place[longest] = (place[longest] + 1) % extent[longest]
    return entries.at[tuple(place)].set(top_value)


def levels(own_key, extent, cuts, least, top_value):
    level, own = 1.0, jax.random.fold_in(own_key, 6)
    for position, blocks in cuts:
        draws = jnp.exp(jax.random.uniform(jax.random.fold_in(own, position), (blocks,), jnp.float32, least / len(cuts), top_value / len(cuts)))
        level = level * jnp.repeat(draws, extent[position] // blocks).reshape([-1 if axis == position else 1 for axis in range(len(extent))])
    return level


def scatter_about(own_key, shape, width, limit, shards=(), kind=jnp.bfloat16):
    level = levels(own_key, shape, shards, -0.22, 0.18) if shards else 1.0
    array = jax.random.normal(own_key, shape, jnp.float32) * width * level
    return jnp.minimum(jnp.maximum(array, -limit), limit).astype(kind)


def setup_inputs(seed: int = 0) -> dict:
    key_list = jax.random.split(jax.random.key(seed), 8)
    peramb = scatter_about(key_list[0], (PAIRS, 2, ORDER, ORDER), 1.0, 6.0, ((0, 128), (3, 8)))
    sink_ops = scatter_about(key_list[1], (PAIRS, NOPS, 2, NV, NV), (2 * NV) ** -0.5, 0.1875, ((0, 128),))
    op_table = scatter_about(key_list[2], (ROWS, 2, NV), (2 * NV) ** -0.5, 0.1875, ((0, 128),))
    row_slot = jax.random.permutation(key_list[3], ROWS).astype(jnp.int32)
    pair_source = with_ends(jax.random.randint(key_list[4], (PAIRS,), 0, NSRC), jax.random.fold_in(key_list[4], 1), 0, NSRC - 1).astype(jnp.int32)
    op_index = with_ends(jax.random.randint(key_list[5], (PROD_ALL, 2), 0, NOPS), jax.random.fold_in(key_list[5], 1), 0, NOPS - 1).astype(jnp.int32)
    listed_rows = with_ends(jax.random.randint(key_list[6], (PROD_ALL, SEL), 0, NV), jax.random.fold_in(key_list[6], 1), 0, NV - 1).astype(jnp.int32)
    return dict(peramb=peramb, sink_ops=sink_ops, op_table=op_table, row_slot=row_slot, pair_source=pair_source, op_index=op_index, listed_rows=listed_rows)


def reference(peramb, sink_ops, op_table, row_slot, pair_source, op_index, listed_rows):
    stored = op_table.astype(jnp.float32)

    def one_product(k):
        pair_id = k // PROD_DEV
        pair = lax.dynamic_index_in_dim(peramb, pair_id, 0, keepdims=False)
        pair = pair.astype(jnp.float32).reshape(2, NS, NV, ORDER)
        chosen = lax.dynamic_index_in_dim(op_index, k, 0, keepdims=False)
        listed = lax.dynamic_index_in_dim(listed_rows, k, 0, keepdims=False)
        sink_all = lax.dynamic_index_in_dim(sink_ops, pair_id, 0, keepdims=False)
        sink_one = lax.dynamic_index_in_dim(sink_all, chosen[0], 0, keepdims=False).astype(jnp.float32)
        left = sink_one[:, listed, :]
        source = lax.dynamic_index_in_dim(pair_source, pair_id, 0, keepdims=False)
        right = stored[row_slot[(source * NOPS + chosen[1]) * NV + jnp.arange(NV, dtype=jnp.int32)]]
        mixed_re = jnp.einsum("iv,svc->sic", left[0], pair[0]) - jnp.einsum("iv,svc->sic", left[1], pair[1])
        mixed_im = jnp.einsum("iv,svc->sic", left[0], pair[1]) + jnp.einsum("iv,svc->sic", left[1], pair[0])
        mixed = jnp.stack([mixed_re, mixed_im]).astype(jnp.bfloat16)
        mixed = lax.optimization_barrier(mixed).astype(jnp.float32).reshape(2, NS, SEL, NS, NV)
        right_re = right[:, 0]
        right_im = right[:, 1]
        out_re = jnp.einsum("sitv,vw->sitw", mixed[0], right_re) - jnp.einsum("sitv,vw->sitw", mixed[1], right_im)
        out_im = jnp.einsum("sitv,vw->sitw", mixed[0], right_im) + jnp.einsum("sitv,vw->sitw", mixed[1], right_re)
        joined = jnp.stack([out_re, out_im], 2).reshape(NS, SEL, 2, ORDER)
        return joined.astype(jnp.bfloat16)

    return lax.map(one_product, jnp.arange(PROD_ALL, dtype=jnp.int32))
```

```python
import jax
import jax.numpy as jnp
from jax import lax
from jax.experimental import pallas as pl
from jax.experimental.pallas import tpu as pltpu
from jax.sharding import PartitionSpec as P

NS = 4
CORES = 2
SIDE = 8
MESH = pl.DeviceIdType.MESH
BF16 = jnp.bfloat16
F32 = jnp.float32


def column_of(row):
    n = row.shape[1]
    return jnp.transpose(jnp.broadcast_to(row, (n, n)))


def onehot_rows(row, width, base=0):
    col = column_of(row)
    n = col.shape[0]
    lane = lax.broadcasted_iota(jnp.int32, (n, n), 1) + base
    parts = [(col == lane + w * n).astype(F32).astype(BF16) for w in range(width // n)]
    return jnp.concatenate(parts, axis=1)


def kernel(
    source_ref, op_ref, listed_ref, slot_ref, peramb_ref, sink_ref, optab_ref, out_ref,
    perv, sinkv, lhs, sendb, recvb, tbl, hot, right, outv,
    in_sem, out_sem, a2a_send, a2a_recv, p1_send, p1_recv, p2_send, p2_recv, fw_send, fw_recv,
):
    nv = sinkv.shape[3]
    n_y = sendb.shape[1]
    own = sendb.shape[2] // (2 * CORES)
    prods = op_ref.shape[0]
    sel = listed_ref.shape[1]
    n = SIDE
    half = n // 2
    t = lax.axis_index("tpair")
    y = lax.axis_index("col")
    c = t % CORES
    x = (t // CORES) % n
    z = t // (CORES * n)
    a = (1 - c) * z + c * x
    b = (1 - c) * x + c * z
    partner = (t + 1 - 2 * c, y)

    def ring_id(a_, b_):
        z_ = (1 - c) * a_ + c * b_
        x_ = (1 - c) * b_ + c * a_
        return ((z_ * n + x_) * CORES + c, y)

    loads = [pltpu.make_async_copy(sink_ref.at[0], sinkv, in_sem.at[0])]
    for s in range(NS):
        for r in range(2):
            loads.append(
                pltpu.make_async_copy(
                    peramb_ref.at[0, r, pl.ds(s * nv, nv)], perv.at[s, r], in_sem.at[1 + s * 2 + r]
                )
            )
    for cp in loads:
        cp.start()

    barrier = pltpu.get_barrier_semaphore()
    peers = [(t, (y + i) % n_y) for i in range(1, n_y)]
    peers += [ring_id(a, (b + i) % n) for i in range(1, n)]
    peers += [ring_id((a + 1) % n, b), ring_id((a + n - 1) % n, b), partner]
    for dev in peers:
        pl.semaphore_signal(barrier, inc=1, device_id=dev, device_id_type=MESH)

    shard = optab_ref[...].astype(F32)
    for r in range(2):
        tbl[c, a, b, r] = shard[:, r, :].astype(BF16)

    row = lax.broadcasted_iota(jnp.int32, (2 * sel, sel), 0)
    col = lax.broadcasted_iota(jnp.int32, (2 * sel, sel), 1)
    even = (row == 2 * col).astype(F32)
    odd = (row == 2 * col + 1).astype(F32)
    spread_a = jnp.concatenate([even, odd], axis=1).astype(BF16)
    spread_b = jnp.concatenate([odd, -even], axis=1).astype(BF16)
    hots = [onehot_rows(listed_ref[k : k + 1, :], nv) for k in range(prods)]
    loads[0].wait()
    for k in range(prods):
        ops = sinkv[op_ref[k, 0]]
        g_re = jnp.dot(hots[k], ops[0], preferred_element_type=F32).astype(BF16)
        g_im = jnp.dot(hots[k], ops[1], preferred_element_type=F32).astype(BF16)
        g = jnp.concatenate([g_re, g_im], axis=0)
        left_a = jnp.dot(spread_a, g, preferred_element_type=F32).astype(BF16)
        left_b = jnp.dot(spread_b, g, preferred_element_type=F32).astype(BF16)
        lhs[:, k, :, 0:nv] = left_a.reshape(n_y, 2 * own, nv)
        lhs[:, k, :, nv : 2 * nv] = left_b.reshape(n_y, 2 * own, nv)

    pl.semaphore_wait(barrier, len(peers))

    phase1 = []
    for i in range(1, n):
        phase1.append(
            pltpu.make_async_remote_copy(
                src_ref=tbl.at[c, a, b], dst_ref=tbl.at[c, a, b],
                send_sem=p1_send.at[i], recv_sem=p1_recv.at[i],
                device_id=ring_id(a, (b + i) % n), device_id_type=MESH,
            )
        )
    for cp in phase1:
        cp.start()

    exchange = []
    for s in range(NS):
        loads[1 + 2 * s].wait()
        loads[2 + 2 * s].wait()
        m = jnp.dot(
            lhs[...].reshape(n_y * prods * 2 * own, 2 * nv),
            perv[s].reshape(2 * nv, perv.shape[3]),
            preferred_element_type=F32,
        )
        sendb[s] = m.astype(BF16).reshape(sendb.shape[1:])
        recvb[s, y] = sendb[s, y]
        for i in range(1, n_y):
            dest = (y + i) % n_y
            cp = pltpu.make_async_remote_copy(
                src_ref=sendb.at[s, dest], dst_ref=recvb.at[s, y],
                send_sem=a2a_send.at[s, i], recv_sem=a2a_recv.at[s, i],
                device_id=(t, dest), device_id_type=MESH,
            )
            cp.start()
            exchange.append(cp)

    for k in range(prods):
        first = source_ref[0] * prods + op_ref[k, 1]
        pos = slot_ref[first]
        pt = pos // 16
        pr = pos % 16
        pc = pt % CORES
        px = (pt // CORES) % n
        pz = pt // (CORES * n)
        pa = (1 - pc) * pz + pc * px
        pb = (1 - pc) * px + pc * pz
        idx = ((pc * n + pa) * n + pb) * 16 + pr
        for j in range(nv // 128):
            hot[pl.ds(k * nv + j * 128, 128), :] = onehot_rows(idx[j : j + 1, :], hot.shape[1])

    for cp in phase1:
        cp.wait_recv()

    plus = ring_id((a + 1) % n, b)
    minus = ring_id((a + n - 1) % n, b)
    phase2 = {}
    forward = {}

    def hop(d, st, h):
        block = (a + n - st + 1) % n if d == 0 else (a + st - 1) % n
        part = tbl.at[c, block, pl.ds(h * half, half)]
        cp = pltpu.make_async_remote_copy(
            src_ref=part, dst_ref=part,
            send_sem=p2_send.at[d, st, h], recv_sem=p2_recv.at[d, st, h],
            device_id=plus if d == 0 else minus, device_id_type=MESH,
        )
        cp.start()
        phase2[d, st, h] = cp

    def pass_on(d, st, h):
        block = (a + n - st) % n if d == 0 else (a + st) % n
        part = tbl.at[c, block, pl.ds(h * half, half)]
        cp = pltpu.make_async_remote_copy(
            src_ref=part, dst_ref=part,
            send_sem=fw_send.at[d, st, h], recv_sem=fw_recv.at[d, st, h],
            device_id=partner, device_id_type=MESH,
        )
        cp.start()
        forward[d, st, h] = cp

    for h in range(2):
        for d in range(2):
            if half > 1 or h == d:
                hop(d, 1, h)
    for h in range(2):
        pass_on(0, 0, h)
    for st in range(1, half + 1):
        for h in range(2):
            for d in range(2):
                if (d, st, h) in phase2:
                    phase2[d, st, h].wait_recv()
                    if st + 1 < half or (st + 1 == half and h == d):
                        hop(d, st + 1, h)
                    pass_on(d, st, h)
    for cp in forward.values():
        cp.wait_recv()

    slots = hot.shape[1]

    def pick(j, carry):
        r = j // 2
        at = pl.ds(pl.multiple_of((j % 2) * (nv // 2), nv // 2), nv // 2)
        rows = tbl[:, :, :, r, :, at].reshape(slots, nv // 2)
        got = jnp.dot(hot[...], rows, preferred_element_type=F32).astype(BF16)
        right[:, :, pl.ds(pl.multiple_of(j * (nv // 2), nv // 2), nv // 2)] = got.reshape(
            prods, nv, nv // 2
        )
        return carry

    lax.fori_loop(0, 4, pick, 0)

    rows = NS * 2 * own
    parity = lax.broadcasted_iota(jnp.int32, (rows, nv), 0) % 2
    stores = []
    per_t = n_y // NS
    for s in range(NS):
        for i in range(1, n_y):
            exchange[s * (n_y - 1) + i - 1].wait_recv()
        for k in range(prods):
            got = recvb[s].reshape(NS, per_t, prods * 2 * own, nv // per_t)
            mixed = jnp.concatenate(
                [
                    got[:, h, k * 2 * own : (k + 1) * 2 * own, :].reshape(rows, nv // per_t)
                    for h in range(per_t)
                ],
                axis=1,
            )
            both = jnp.dot(mixed, right[k], preferred_element_type=F32)
            by_re = both[:, :nv]
            by_im = both[:, nv:]
            turned = jnp.where(
                parity == 0, -pltpu.roll(by_im, rows - 1, 0), pltpu.roll(by_im, 1, 0)
            )
            res = (by_re + turned).astype(BF16)
            for tt in range(NS):
                outv[k, s, :, tt * nv : (tt + 1) * nv] = res[tt * 2 * own : (tt + 1) * 2 * own]
            cp = pltpu.make_async_copy(outv.at[k, s], out_ref.at[k, s], out_sem.at[k, s])
            cp.start()
            stores.append(cp)

    for cp in phase1 + exchange + list(phase2.values()) + list(forward.values()):
        cp.wait_send()
    for cp in stores:
        cp.wait()


def per_device(peramb, sink_ops, op_table, row_slot, pair_source, op_index, listed_rows):
    n_y = lax.axis_size("col")
    nv = op_table.shape[2]
    cols = peramb.shape[3]
    prods, sel = listed_rows.shape
    own = sel // n_y
    shard = op_table.shape[0]
    order = NS * nv
    slots = lax.axis_size("tpair") * shard
    half = SIDE // 2
    dma = pltpu.SemaphoreType.DMA
    vmem = pl.BlockSpec(memory_space=pltpu.VMEM)
    smem = pl.BlockSpec(memory_space=pltpu.SMEM)
    hbm = pl.BlockSpec(memory_space=pl.ANY)
    out = pl.pallas_call(
        kernel,
        out_shape=jax.ShapeDtypeStruct((prods, NS, 2 * own, order), BF16),
        in_specs=[smem, smem, vmem, vmem, hbm, hbm, vmem],
        out_specs=hbm,
        scratch_shapes=[
            pltpu.VMEM((NS, 2, nv, cols), BF16),
            pltpu.VMEM(sink_ops.shape[1:], BF16),
            pltpu.VMEM((n_y, prods, 2 * own, 2 * nv), BF16),
            pltpu.VMEM((NS, n_y, prods * 2 * own, cols), BF16),
            pltpu.VMEM((NS, n_y, prods * 2 * own, cols), BF16),
            pltpu.VMEM((CORES, SIDE, SIDE, 2, shard, nv), BF16),
            pltpu.VMEM((prods * nv, slots), BF16),
            pltpu.VMEM((prods, nv, 2 * nv), BF16),
            pltpu.VMEM((prods, NS, 2 * own, order), BF16),
            dma((1 + 2 * NS,)),
            dma((prods, NS)),
            dma((NS, n_y)),
            dma((NS, n_y)),
            dma((SIDE,)),
            dma((SIDE,)),
            dma((2, half + 1, 2)),
            dma((2, half + 1, 2)),
            dma((2, half + 1, 2)),
            dma((2, half + 1, 2)),
        ],
        compiler_params=pltpu.CompilerParams(
            collective_id=0, has_side_effects=True, vmem_limit_bytes=56 << 20
        ),
        name="contract",
    )(
        pair_source,
        op_index,
        listed_rows,
        row_slot.reshape(-1, nv // 128, 128),
        peramb,
        sink_ops,
        op_table,
    )
    return out.reshape(prods, NS, own, 2, order)


def solution(mesh):
    in_specs = (
        P("tpair", None, None, "col"),
        P("tpair", None, None, None, None),
        P("tpair", None, None),
        P(),
        P("tpair"),
        P("tpair", None),
        P("tpair", None),
    )
    out_specs = P("tpair", None, "col", None, None)
    return jax.shard_map(
        per_device, mesh=mesh, in_specs=in_specs, out_specs=out_specs, check_vma=False
    )
```

```python
import jax
import jax.numpy as jnp
from jax import lax
from jax.experimental import pallas as pl
from jax.experimental.pallas import tpu as pltpu
from jax.sharding import PartitionSpec as P

NS = 4
CORES = 2
SIDE = 8
MESH = pl.DeviceIdType.MESH
BF16 = jnp.bfloat16
F32 = jnp.float32


def column_of(row):
    n = row.shape[1]
    return jnp.transpose(jnp.broadcast_to(row, (n, n)))


def onehot_rows(row, width, base=0):
    col = column_of(row)
    n = col.shape[0]
    lane = lax.broadcasted_iota(jnp.int32, (n, n), 1) + base
    parts = [(col == lane + w * n).astype(F32).astype(BF16) for w in range(width // n)]
    return jnp.concatenate(parts, axis=1)


def kernel(
    source_ref, op_ref, listed_ref, slot_ref, peramb_ref, sink_ref, optab_ref, out_ref,
    perv, sinkv, lhs, sendb, recvb, tbl, hot, right,
    in_sem, a2a_send, a2a_recv, p1_send, p1_recv, hop_send, hop_recv, fw_send, fw_recv,
    ready_y, ready_z, ready_x, ready_c,
):
    nv = sinkv.shape[3]
    n_y = sendb.shape[1]
    own = sendb.shape[2] // (2 * CORES)
    prods = op_ref.shape[0]
    sel = listed_ref.shape[1]
    n = SIDE
    half = n // 2
    quarters = n // 2
    t = lax.axis_index("tpair")
    y = lax.axis_index("col")
    c = t % CORES
    x = (t // CORES) % n
    z = t // (CORES * n)

    def at_z(i):
        return ((((z + i) % n) * n + x) * CORES + c, y)

    def at_x(i):
        return ((z * n + (x + i) % n) * CORES + c, y)

    def at_y(i):
        return (t, (y + i) % n_y)

    partner = (t + 1 - 2 * c, y)

    loads = [pltpu.make_async_copy(sink_ref.at[0], sinkv, in_sem.at[0])]
    for s in range(NS):
        for r in range(2):
            loads.append(
                pltpu.make_async_copy(
                    peramb_ref.at[0, r, pl.ds(s * nv, nv)], perv.at[s, r], in_sem.at[1 + s * 2 + r]
                )
            )
    for cp in loads:
        cp.start()

    peers = []
    for i in range(1, n_y):
        peers.append((at_y(i), y + i < n_y, ready_y.at[i], ready_y.at[n_y - i]))
    for i in range(1, n):
        peers.append((at_z(i), z + i < n, ready_z.at[i], ready_z.at[n - i]))
    for i in (1, n - 1):
        peers.append((at_x(i), x + i < n, ready_x.at[i], ready_x.at[n - i]))
    peers.append((partner, c == 1, ready_c.at[0], ready_c.at[0]))
    barrier = pltpu.get_barrier_semaphore()
    for dev, later, _, _ in peers:

        @pl.when(later)
        def _(dev=dev):
            pl.semaphore_signal(barrier, inc=1, device_id=dev, device_id_type=MESH)

    shard = optab_ref[...].astype(F32)
    for r in range(2):
        tbl[z, x, c, r] = shard[:, r, :].astype(BF16)

    earlier = y + z + (x + n - 1) // n + (x + 1) // n + 1 - c

    @pl.when(earlier > 0)
    def _():
        pl.semaphore_wait(barrier, earlier)

    for dev, later, _, theirs in peers:

        @pl.when(jnp.logical_not(later))
        def _(dev=dev, theirs=theirs):
            pl.semaphore_signal(theirs, inc=1, device_id=dev, device_id_type=MESH)

    def await_answer(index):
        _, later, mine, _ = peers[index]

        @pl.when(later)
        def _():
            pl.semaphore_wait(mine, 1)

    def shard_copy(i):
        return pltpu.make_async_remote_copy(
            src_ref=tbl.at[z, x, c], dst_ref=tbl.at[z, x, c],
            send_sem=p1_send.at[i], recv_sem=p1_recv.at[i],
            device_id=at_z(i), device_id_type=MESH,
        )

    phase1 = [None] + [shard_copy(i) for i in range(1, n)]
    for i in range(1, n):

        @pl.when(z + i >= n)
        def _(i=i):
            phase1[i].start()

    row = lax.broadcasted_iota(jnp.int32, (2 * sel, sel), 0)
    col = lax.broadcasted_iota(jnp.int32, (2 * sel, sel), 1)
    even = (row == 2 * col).astype(F32)
    odd = (row == 2 * col + 1).astype(F32)
    spread_a = jnp.concatenate([even, odd], axis=1).astype(BF16)
    spread_b = jnp.concatenate([odd, -even], axis=1).astype(BF16)
    hots = [onehot_rows(listed_ref[k : k + 1, :], nv) for k in range(prods)]
    loads[0].wait()
    for k in range(prods):
        ops = sinkv[op_ref[k, 0]]
        g_re = jnp.dot(hots[k], ops[0], preferred_element_type=F32).astype(BF16)
        g_im = jnp.dot(hots[k], ops[1], preferred_element_type=F32).astype(BF16)
        g = jnp.concatenate([g_re, g_im], axis=0)
        left_a = jnp.dot(spread_a, g, preferred_element_type=F32).astype(BF16)
        left_b = jnp.dot(spread_b, g, preferred_element_type=F32).astype(BF16)
        lhs[:, k, :, 0:nv] = left_a.reshape(n_y, 2 * own, nv)
        lhs[:, k, :, nv : 2 * nv] = left_b.reshape(n_y, 2 * own, nv)

    exchange = []
    for s in range(NS):
        loads[1 + 2 * s].wait()
        loads[2 + 2 * s].wait()
        m = jnp.dot(
            lhs[...].reshape(n_y * prods * 2 * own, 2 * nv),
            perv[s].reshape(2 * nv, perv.shape[3]),
            preferred_element_type=F32,
        )
        sendb[s] = m.astype(BF16).reshape(sendb.shape[1:])
        recvb[s, y] = sendb[s, y]
        for i in range(1, n_y):
            if s == 0:
                await_answer(i - 1)
            cp = pltpu.make_async_remote_copy(
                src_ref=sendb.at[s, (y + i) % n_y], dst_ref=recvb.at[s, y],
                send_sem=a2a_send.at[s, i], recv_sem=a2a_recv.at[s, i],
                device_id=at_y(i), device_id_type=MESH,
            )
            cp.start()
            exchange.append(cp)

    for k in range(prods):
        pos = slot_ref[source_ref[0] * prods + op_ref[k, 1]]
        for j in range(nv // 128):
            hot[pl.ds(k * nv + j * 128, 128), :] = onehot_rows(pos[j : j + 1, :], hot.shape[1])

    hops = {}
    forward = {}

    def piece(q, d, st, block):
        if st < half:
            return tbl.at[pl.ds(2 * q, 2), block, c]
        return tbl.at[pl.ds(2 * q + d, 1), block, c]

    def hop(q, d, st):
        part = piece(q, d, st, (x + n - st + 1) % n if d == 0 else (x + st - 1) % n)
        cp = pltpu.make_async_remote_copy(
            src_ref=part, dst_ref=part,
            send_sem=hop_send.at[q, d, st], recv_sem=hop_recv.at[q, d, st],
            device_id=at_x(1 if d == 0 else n - 1), device_id_type=MESH,
        )
        cp.start()
        hops[q, d, st] = cp

    def pass_on(q, d, st):
        part = piece(q, d, st, (x + n - st) % n if d == 0 else (x + st) % n)
        cp = pltpu.make_async_remote_copy(
            src_ref=part, dst_ref=part,
            send_sem=fw_send.at[q, d, st], recv_sem=fw_recv.at[q, d, st],
            device_id=partner, device_id_type=MESH,
        )
        cp.start()
        forward[q, d, st] = cp

    def open_pair(q):
        for w in (2 * q, 2 * q + 1):
            for i in range(1, n):
                if i <= w:

                    @pl.when(z + i == w)
                    def _(i=i):
                        pl.semaphore_wait(ready_z.at[i], 1)
                        phase1[i].start()

        for w in (2 * q, 2 * q + 1):
            for i in range(1, n):

                @pl.when((w + i) % n == z)
                def _(i=i):
                    phase1[i].wait_recv()

        if q == 0:
            await_answer(n_y - 1 + n - 1)
            await_answer(n_y - 1 + n)
        for d in range(2):
            hop(q, d, 1)
        if q == 0:
            await_answer(n_y - 1 + n + 1)
        pass_on(q, 0, 0)

    def relay(q, st):
        for d in range(2):
            hops[q, d, st].wait_recv()
            if st < half:
                hop(q, d, st + 1)
            pass_on(q, d, st)

    def pick(q):
        for d in range(2):
            for st in range(half + 1):
                if (q, d, st) in forward:
                    forward[q, d, st].wait_recv()
        span = hot.shape[1] // quarters
        width = nv // 2

        def column(j, carry):
            at = pl.ds(pl.multiple_of((j % 2) * width, width), width)
            rows = tbl[2 * q : 2 * q + 2, :, :, j // 2, :, at].reshape(span, width)
            got = jnp.dot(
                hot[:, q * span : (q + 1) * span], rows, preferred_element_type=F32
            ).astype(BF16).reshape(prods, nv, width)
            to = pl.ds(pl.multiple_of(j * width, width), width)
            if q == 0:
                right[:, :, to] = got
            else:
                right[:, :, to] = right[:, :, to] + got
            return carry

        lax.fori_loop(0, 4, column, 0)

    open_pair(0)
    relay(0, 1)
    relay(0, 2)
    open_pair(1)
    relay(0, 3)
    relay(1, 1)
    relay(0, 4)
    relay(1, 2)
    pick(0)
    open_pair(2)
    relay(1, 3)
    relay(2, 1)
    open_pair(3)
    relay(1, 4)
    relay(2, 2)
    pick(1)
    relay(3, 1)
    relay(2, 3)
    relay(3, 2)
    relay(2, 4)
    pick(2)
    relay(3, 3)
    relay(3, 4)
    pick(3)

    for cp in exchange:
        cp.wait_recv()
    per_t = n_y // NS
    group = NS // 2
    rows = group * NS * 2 * own
    parity = lax.broadcasted_iota(jnp.int32, (rows, nv), 0) % 2
    for k in range(prods):
        for m in range(2):
            got = recvb[m * group : (m + 1) * group].reshape(
                group * NS, per_t, prods * 2 * own, nv // per_t
            )
            mixed = jnp.concatenate(
                [
                    got[:, h, k * 2 * own : (k + 1) * 2 * own, :].reshape(rows, nv // per_t)
                    for h in range(per_t)
                ],
                axis=1,
            )
            both = jnp.dot(mixed, right[k], preferred_element_type=F32)
            by_re = both[:, :nv]
            by_im = both[:, nv:]
            turned = jnp.where(
                parity == 0, -pltpu.roll(by_im, rows - 1, 0), pltpu.roll(by_im, 1, 0)
            )
            res = (by_re + turned).astype(BF16).reshape(group, NS, 2 * own, nv)
            for tt in range(NS):
                out_ref[k, m * group : (m + 1) * group, :, tt * nv : (tt + 1) * nv] = res[:, tt]

    for cp in phase1[1:] + exchange + list(hops.values()) + list(forward.values()):
        cp.wait_send()


def per_device(peramb, sink_ops, op_table, row_slot, pair_source, op_index, listed_rows):
    n_y = lax.axis_size("col")
    nv = op_table.shape[2]
    cols = peramb.shape[3]
    prods, sel = listed_rows.shape
    own = sel // n_y
    shard = op_table.shape[0]
    order = NS * nv
    slots = lax.axis_size("tpair") * shard
    half = SIDE // 2
    dma = pltpu.SemaphoreType.DMA
    vmem = pl.BlockSpec(memory_space=pltpu.VMEM)
    smem = pl.BlockSpec(memory_space=pltpu.SMEM)
    hbm = pl.BlockSpec(memory_space=pl.ANY)
    out = pl.pallas_call(
        kernel,
        out_shape=pltpu.VMEM((prods, NS, 2 * own, order), BF16),
        in_specs=[smem, smem, vmem, vmem, hbm, hbm, vmem],
        out_specs=vmem,
        scratch_shapes=[
            pltpu.VMEM((NS, 2, nv, cols), BF16),
            pltpu.VMEM(sink_ops.shape[1:], BF16),
            pltpu.VMEM((n_y, prods, 2 * own, 2 * nv), BF16),
            pltpu.VMEM((NS, n_y, prods * 2 * own, cols), BF16),
            pltpu.VMEM((NS, n_y, prods * 2 * own, cols), BF16),
            pltpu.VMEM((SIDE, SIDE, CORES, 2, shard, nv), BF16),
            pltpu.VMEM((prods * nv, slots), BF16),
            pltpu.VMEM((prods, nv, 2 * nv), BF16),
            dma((1 + 2 * NS,)),
            dma((NS, n_y)),
            dma((NS, n_y)),
            dma((SIDE,)),
            dma((SIDE,)),
            dma((half, 2, half + 1)),
            dma((half, 2, half + 1)),
            dma((half, 2, half + 1)),
            dma((half, 2, half + 1)),
            pltpu.SemaphoreType.REGULAR((n_y,)),
            pltpu.SemaphoreType.REGULAR((SIDE,)),
            pltpu.SemaphoreType.REGULAR((SIDE,)),
            pltpu.SemaphoreType.REGULAR((1,)),
        ],
        compiler_params=pltpu.CompilerParams(
            collective_id=0, has_side_effects=True, vmem_limit_bytes=56 << 20
        ),
        name="contract",
    )(
        pair_source,
        op_index,
        listed_rows,
        row_slot.reshape(-1, nv // 128, 128),
        peramb,
        sink_ops,
        op_table,
    )
    return out.reshape(prods, NS, own, 2, order)


def solution(mesh):
    in_specs = (
        P("tpair", None, None, "col"),
        P("tpair", None, None, None, None),
        P("tpair", None, None),
        P(),
        P("tpair"),
        P("tpair", None),
        P("tpair", None),
    )
    out_specs = P("tpair", None, "col", None, None)
    return jax.shard_map(
        per_device, mesh=mesh, in_specs=in_specs, out_specs=out_specs, check_vma=False
    )
```

```python
import jax
import jax.numpy as jnp
from jax import lax
from jax.experimental import pallas as pl
from jax.experimental.pallas import tpu as pltpu
from jax.sharding import PartitionSpec as P

NS = 4
CORES = 2
SIDE = 8
MESH = pl.DeviceIdType.MESH
BF16 = jnp.bfloat16
F32 = jnp.float32


def column_of(row):
    n = row.shape[1]
    return jnp.transpose(jnp.broadcast_to(row, (n, n)))


def onehot_rows(row, width, base=0):
    col = column_of(row)
    n = col.shape[0]
    lane = lax.broadcasted_iota(jnp.int32, (n, n), 1) + base
    parts = [(col == lane + w * n).astype(F32).astype(BF16) for w in range(width // n)]
    return jnp.concatenate(parts, axis=1)


def kernel(
    source_ref, op_ref, listed_ref, slot_ref, peramb_ref, sink_ref, optab_ref, out_ref,
    perv, sinkv, lhs, sendb, recvb, tbl, hot, right,
    in_sem, a2a_send, a2a_recv, p1_send, p1_recv, hop_send, hop_recv, fw_send, fw_recv,
    ready_y, ready_b, ready_a, ready_c,
):
    nv = sinkv.shape[3]
    n_y = sendb.shape[1]
    own = sendb.shape[2] // (2 * CORES)
    prods = op_ref.shape[0]
    sel = listed_ref.shape[1]
    n = SIDE
    half = n // 2
    t = lax.axis_index("tpair")
    y = lax.axis_index("col")
    c = t % CORES
    x = (t // CORES) % n
    z = t // (CORES * n)

    a = (1 - c) * z + c * x
    b = (1 - c) * x + c * z

    def ring_id(a_, b_):
        z_ = (1 - c) * a_ + c * b_
        x_ = (1 - c) * b_ + c * a_
        return ((z_ * n + x_) * CORES + c, y)

    def first_axis(i):
        return ring_id(a, (b + i) % n)

    def second_axis(i):
        return ring_id((a + i) % n, b)

    def at_y(i):
        return (t, (y + i) % n_y)

    partner = (t + 1 - 2 * c, y)

    loads = [pltpu.make_async_copy(sink_ref.at[0], sinkv, in_sem.at[0])]
    for s in range(NS):
        for r in range(2):
            loads.append(
                pltpu.make_async_copy(
                    peramb_ref.at[0, r, pl.ds(s * nv, nv)], perv.at[s, r], in_sem.at[1 + s * 2 + r]
                )
            )
    for cp in loads:
        cp.start()

    peers = []
    for i in range(1, n_y):
        peers.append((at_y(i), y + i < n_y, ready_y.at[i], ready_y.at[n_y - i]))
    for i in range(1, n):
        peers.append((first_axis(i), b + i < n, ready_b.at[i], ready_b.at[n - i]))
    for i in (1, n - 1):
        peers.append((second_axis(i), a + i < n, ready_a.at[i], ready_a.at[n - i]))
    peers.append((partner, c == 1, ready_c.at[0], ready_c.at[0]))
    barrier = pltpu.get_barrier_semaphore()
    for dev, later, _, _ in peers:

        @pl.when(later)
        def _(dev=dev):
            pl.semaphore_signal(barrier, inc=1, device_id=dev, device_id_type=MESH)

    shard = optab_ref[...].astype(F32)
    for r in range(2):
        tbl[c, a, b, r] = shard[:, r, :].astype(BF16)

    earlier = y + b + (a + n - 1) // n + (a + 1) // n + 1 - c

    @pl.when(earlier > 0)
    def _():
        pl.semaphore_wait(barrier, earlier)

    for dev, later, _, theirs in peers:

        @pl.when(jnp.logical_not(later))
        def _(dev=dev, theirs=theirs):
            pl.semaphore_signal(theirs, inc=1, device_id=dev, device_id_type=MESH)

    def await_answer(index):
        _, later, mine, _ = peers[index]

        @pl.when(later)
        def _():
            pl.semaphore_wait(mine, 1)

    def shard_copy(i):
        return pltpu.make_async_remote_copy(
            src_ref=tbl.at[c, a, b], dst_ref=tbl.at[c, a, b],
            send_sem=p1_send.at[i], recv_sem=p1_recv.at[i],
            device_id=first_axis(i), device_id_type=MESH,
        )

    phase1 = [None] + [shard_copy(i) for i in range(1, n)]
    for i in range(1, n):

        @pl.when(b + i >= n)
        def _(i=i):
            phase1[i].start()

    @pl.when(c == 0)
    def _():
        for i in range(1, n):

            @pl.when(b + i < n)
            def _(i=i):
                pl.semaphore_wait(ready_b.at[i], 1)
                phase1[i].start()

    row = lax.broadcasted_iota(jnp.int32, (2 * sel, sel), 0)
    col = lax.broadcasted_iota(jnp.int32, (2 * sel, sel), 1)
    even = (row == 2 * col).astype(F32)
    odd = (row == 2 * col + 1).astype(F32)
    spread_a = jnp.concatenate([even, odd], axis=1).astype(BF16)
    spread_b = jnp.concatenate([odd, -even], axis=1).astype(BF16)
    hots = [onehot_rows(listed_ref[k : k + 1, :], nv) for k in range(prods)]
    loads[0].wait()
    for k in range(prods):
        ops = sinkv[op_ref[k, 0]]
        g_re = jnp.dot(hots[k], ops[0], preferred_element_type=F32).astype(BF16)
        g_im = jnp.dot(hots[k], ops[1], preferred_element_type=F32).astype(BF16)
        g = jnp.concatenate([g_re, g_im], axis=0)
        left_a = jnp.dot(spread_a, g, preferred_element_type=F32).astype(BF16)
        left_b = jnp.dot(spread_b, g, preferred_element_type=F32).astype(BF16)
        lhs[:, k, :, 0:nv] = left_a.reshape(n_y, 2 * own, nv)
        lhs[:, k, :, nv : 2 * nv] = left_b.reshape(n_y, 2 * own, nv)

    exchange = []
    for s in range(NS):
        loads[1 + 2 * s].wait()
        loads[2 + 2 * s].wait()
        m = jnp.dot(
            lhs[...].reshape(n_y * prods * 2 * own, 2 * nv),
            perv[s].reshape(2 * nv, perv.shape[3]),
            preferred_element_type=F32,
        )
        sendb[s] = m.astype(BF16).reshape(sendb.shape[1:])
        recvb[s, y] = sendb[s, y]
        for i in range(1, n_y):
            if s == 0:
                await_answer(i - 1)
            cp = pltpu.make_async_remote_copy(
                src_ref=sendb.at[s, (y + i) % n_y], dst_ref=recvb.at[s, y],
                send_sem=a2a_send.at[s, i], recv_sem=a2a_recv.at[s, i],
                device_id=at_y(i), device_id_type=MESH,
            )
            cp.start()
            exchange.append(cp)

    for k in range(prods):
        pos = slot_ref[source_ref[0] * prods + op_ref[k, 1]]
        pt = pos // 16
        pc = pt % CORES
        px = (pt // CORES) % n
        pz = pt // (CORES * n)
        pa = (1 - pc) * pz + pc * px
        pb = (1 - pc) * px + pc * pz
        idx = ((pc * n + pa) * n + pb) * 16 + pos % 16
        for j in range(nv // 128):
            hot[pl.ds(k * nv + j * 128, 128), :] = onehot_rows(idx[j : j + 1, :], hot.shape[1])

    @pl.when(c == 1)
    def _():
        for i in range(1, n):

            @pl.when(b + i < n)
            def _(i=i):
                pl.semaphore_wait(ready_b.at[i], 1)
                phase1[i].start()

    for cp in phase1[1:]:
        cp.wait_recv()

    hops = {}
    forward = {}

    def hop(d, st, h):
        part = tbl.at[c, (a + n - st + 1) % n if d == 0 else (a + st - 1) % n, pl.ds(h * half, half)]
        cp = pltpu.make_async_remote_copy(
            src_ref=part, dst_ref=part,
            send_sem=hop_send.at[d, st, h], recv_sem=hop_recv.at[d, st, h],
            device_id=second_axis(1 if d == 0 else n - 1), device_id_type=MESH,
        )
        cp.start()
        hops[d, st, h] = cp

    def pass_on(d, st, h):
        part = tbl.at[c, (a + n - st) % n if d == 0 else (a + st) % n, pl.ds(h * half, half)]
        cp = pltpu.make_async_remote_copy(
            src_ref=part, dst_ref=part,
            send_sem=fw_send.at[d, st, h], recv_sem=fw_recv.at[d, st, h],
            device_id=partner, device_id_type=MESH,
        )
        cp.start()
        forward[d, st, h] = cp

    def relay(st):
        for h in range(2):
            for d in range(2):
                if (d, st, h) in hops:
                    hops[d, st, h].wait_recv()
                    if st + 1 < half or (st + 1 == half and h == d):
                        hop(d, st + 1, h)
                    pass_on(d, st, h)

    span = n * 16
    width = nv // 2

    def pick(st):
        for d in range(2):
            for h in range(2):
                if (d, st, h) in forward:
                    forward[d, st, h].wait_recv()
        blocks = []
        for core, at in ((c, a), (1 - c, b)):
            for i in (st, n - st) if 0 < st < half else (st,):
                blocks.append((core, (at + i) % n))
        pairs = [blocks[i : i + 2] for i in range(0, len(blocks), 2)]

        def column(j, carry):
            at = pl.ds(pl.multiple_of((j % 2) * width, width), width)
            got = None
            for pair in pairs:
                left = jnp.concatenate(
                    [
                        hot[:, pl.ds(pl.multiple_of((core * n + blk) * span, span), span)]
                        for core, blk in pair
                    ],
                    axis=1,
                )
                rows = jnp.concatenate(
                    [tbl[core, blk, :, j // 2, :, at].reshape(span, width) for core, blk in pair],
                    axis=0,
                )
                part = jnp.dot(left, rows, preferred_element_type=F32)
                got = part if got is None else got + part
            got = got.astype(BF16).reshape(prods, nv, width)
            to = pl.ds(pl.multiple_of(j * width, width), width)
            if st == 0:
                right[:, :, to] = got
            else:
                right[:, :, to] = right[:, :, to] + got
            return carry

        lax.fori_loop(0, 4, column, 0)

    await_answer(n_y - 1 + n - 1)
    for h in range(2):
        hop(0, 1, h)
    await_answer(n_y - 1 + n + 1)
    for h in range(2):
        pass_on(0, 0, h)
    await_answer(n_y - 1 + n)
    for h in range(2):
        hop(1, 1, h)
    relay(1)
    pick(0)
    relay(2)
    pick(1)
    relay(3)
    pick(2)
    relay(4)
    pick(3)
    pick(4)

    for cp in exchange:
        cp.wait_recv()
    per_t = n_y // NS
    group = NS // 2
    rows = group * NS * 2 * own
    parity = lax.broadcasted_iota(jnp.int32, (rows, nv), 0) % 2
    for k in range(prods):
        for m in range(2):
            got = recvb[m * group : (m + 1) * group].reshape(
                group * NS, per_t, prods * 2 * own, nv // per_t
            )
            mixed = jnp.concatenate(
                [
                    got[:, h, k * 2 * own : (k + 1) * 2 * own, :].reshape(rows, nv // per_t)
                    for h in range(per_t)
                ],
                axis=1,
            )
            both = jnp.dot(mixed, right[k], preferred_element_type=F32)
            by_re = both[:, :nv]
            by_im = both[:, nv:]
            turned = jnp.where(
                parity == 0, -pltpu.roll(by_im, rows - 1, 0), pltpu.roll(by_im, 1, 0)
            )
            res = (by_re + turned).astype(BF16).reshape(group, NS, 2 * own, nv)
            for tt in range(NS):
                out_ref[k, m * group : (m + 1) * group, :, tt * nv : (tt + 1) * nv] = res[:, tt]

    for cp in phase1[1:] + exchange + list(hops.values()) + list(forward.values()):
        cp.wait_send()


def per_device(peramb, sink_ops, op_table, row_slot, pair_source, op_index, listed_rows):
    n_y = lax.axis_size("col")
    nv = op_table.shape[2]
    cols = peramb.shape[3]
    prods, sel = listed_rows.shape
    own = sel // n_y
    shard = op_table.shape[0]
    order = NS * nv
    slots = lax.axis_size("tpair") * shard
    half = SIDE // 2
    dma = pltpu.SemaphoreType.DMA
    vmem = pl.BlockSpec(memory_space=pltpu.VMEM)
    smem = pl.BlockSpec(memory_space=pltpu.SMEM)
    hbm = pl.BlockSpec(memory_space=pl.ANY)
    out = pl.pallas_call(
        kernel,
        out_shape=pltpu.VMEM((prods, NS, 2 * own, order), BF16),
        in_specs=[smem, smem, vmem, vmem, hbm, hbm, vmem],
        out_specs=vmem,
        scratch_shapes=[
            pltpu.VMEM((NS, 2, nv, cols), BF16),
            pltpu.VMEM(sink_ops.shape[1:], BF16),
            pltpu.VMEM((n_y, prods, 2 * own, 2 * nv), BF16),
            pltpu.VMEM((NS, n_y, prods * 2 * own, cols), BF16),
            pltpu.VMEM((NS, n_y, prods * 2 * own, cols), BF16),
            pltpu.VMEM((CORES, SIDE, SIDE, 2, shard, nv), BF16),
            pltpu.VMEM((prods * nv, slots), BF16),
            pltpu.VMEM((prods, nv, 2 * nv), BF16),
            dma((1 + 2 * NS,)),
            dma((NS, n_y)),
            dma((NS, n_y)),
            dma((SIDE,)),
            dma((SIDE,)),
            dma((2, half + 1, 2)),
            dma((2, half + 1, 2)),
            dma((2, half + 1, 2)),
            dma((2, half + 1, 2)),
            pltpu.SemaphoreType.REGULAR((n_y,)),
            pltpu.SemaphoreType.REGULAR((SIDE,)),
            pltpu.SemaphoreType.REGULAR((SIDE,)),
            pltpu.SemaphoreType.REGULAR((1,)),
        ],
        compiler_params=pltpu.CompilerParams(
            collective_id=0, has_side_effects=True, vmem_limit_bytes=56 << 20
        ),
        name="contract",
    )(
        pair_source,
        op_index,
        listed_rows,
        row_slot.reshape(-1, nv // 128, 128),
        peramb,
        sink_ops,
        op_table,
    )
    return out.reshape(prods, NS, own, 2, order)


def solution(mesh):
    in_specs = (
        P("tpair", None, None, "col"),
        P("tpair", None, None, None, None),
        P("tpair", None, None),
        P(),
        P("tpair"),
        P("tpair", None),
        P("tpair", None),
    )
    out_specs = P("tpair", None, "col", None, None)
    return jax.shard_map(
        per_device, mesh=mesh, in_specs=in_specs, out_specs=out_specs, check_vma=False
    )
```

```python
import jax
import jax.numpy as jnp
from jax import lax
from jax.experimental import pallas as pl
from jax.experimental.pallas import tpu as pltpu
from jax.sharding import PartitionSpec as P

NS = 4
CORES = 2
SIDE = 8
MESH = pl.DeviceIdType.MESH
BF16 = jnp.bfloat16
F32 = jnp.float32


def column_of(row):
    n = row.shape[1]
    return jnp.transpose(jnp.broadcast_to(row, (n, n)))


def onehot_rows(row, width, base=0):
    col = column_of(row)
    n = col.shape[0]
    lane = lax.broadcasted_iota(jnp.int32, (n, n), 1) + base
    parts = [(col == lane + w * n).astype(F32).astype(BF16) for w in range(width // n)]
    return jnp.concatenate(parts, axis=1)


def kernel(
    source_ref, op_ref, listed_ref, slot_ref, peramb_ref, sink_ref, optab_ref, out_ref,
    perv, sinkv, lhs, sendb, recvb, tbl, hot, right,
    in_sem, a2a_send, a2a_recv, p1_send, p1_recv, hop_send, hop_recv, fw_send, fw_recv,
    ready_y, ready_b, ready_a, ready_c,
):
    nv = sinkv.shape[3]
    n_y = sendb.shape[1]
    own = sendb.shape[2] // (2 * CORES)
    prods = op_ref.shape[0]
    sel = listed_ref.shape[1]
    n = SIDE
    half = n // 2
    t = lax.axis_index("tpair")
    y = lax.axis_index("col")
    c = t % CORES
    x = (t // CORES) % n
    z = t // (CORES * n)

    a = (1 - c) * z + c * x
    b = (1 - c) * x + c * z

    def ring_id(a_, b_):
        z_ = (1 - c) * a_ + c * b_
        x_ = (1 - c) * b_ + c * a_
        return ((z_ * n + x_) * CORES + c, y)

    def first_axis(i):
        return ring_id(a, (b + i) % n)

    def second_axis(i):
        return ring_id((a + i) % n, b)

    def at_y(i):
        return (t, (y + i) % n_y)

    partner = (t + 1 - 2 * c, y)

    loads = [pltpu.make_async_copy(sink_ref.at[0], sinkv, in_sem.at[0])]
    for s in range(NS):
        for r in range(2):
            loads.append(
                pltpu.make_async_copy(
                    peramb_ref.at[0, r, pl.ds(s * nv, nv)], perv.at[s, r], in_sem.at[1 + s * 2 + r]
                )
            )
    for cp in loads:
        cp.start()

    peers = []
    for i in range(1, n_y):
        peers.append((at_y(i), y + i < n_y, ready_y.at[i], ready_y.at[n_y - i]))
    for i in range(1, n):
        peers.append((first_axis(i), b + i < n, ready_b.at[i], ready_b.at[n - i]))
    for i in (1, n - 1):
        peers.append((second_axis(i), a + i < n, ready_a.at[i], ready_a.at[n - i]))
    peers.append((partner, c == 1, ready_c.at[0], ready_c.at[0]))
    barrier = pltpu.get_barrier_semaphore()
    for dev, later, _, _ in peers:

        @pl.when(later)
        def _(dev=dev):
            pl.semaphore_signal(barrier, inc=1, device_id=dev, device_id_type=MESH)

    shard = optab_ref[...].astype(F32)
    for r in range(2):
        tbl[c, a, b, r] = shard[:, r, :].astype(BF16)

    earlier = y + b + (a + n - 1) // n + (a + 1) // n + 1 - c

    @pl.when(earlier > 0)
    def _():
        pl.semaphore_wait(barrier, earlier)

    for dev, later, _, theirs in peers:

        @pl.when(jnp.logical_not(later))
        def _(dev=dev, theirs=theirs):
            pl.semaphore_signal(theirs, inc=1, device_id=dev, device_id_type=MESH)

    def await_answer(index):
        _, later, mine, _ = peers[index]

        @pl.when(later)
        def _():
            pl.semaphore_wait(mine, 1)

    def shard_copy(i):
        return pltpu.make_async_remote_copy(
            src_ref=tbl.at[c, a, b], dst_ref=tbl.at[c, a, b],
            send_sem=p1_send.at[i], recv_sem=p1_recv.at[i],
            device_id=first_axis(i), device_id_type=MESH,
        )

    phase1 = [None] + [shard_copy(i) for i in range(1, n)]
    for i in range(1, n):

        @pl.when(b + i >= n)
        def _(i=i):
            phase1[i].start()

    @pl.when(c == 0)
    def _():
        for i in range(1, n):

            @pl.when(b + i < n)
            def _(i=i):
                pl.semaphore_wait(ready_b.at[i], 1)
                phase1[i].start()

    hops = {}
    forward = {}

    def hop(p, d, st):
        part = tbl.at[c, (a + n - st + 1) % n if d == 0 else (a + st - 1) % n, (b + n - p) % n]
        hops[p, d, st] = pltpu.make_async_remote_copy(
            src_ref=part, dst_ref=part,
            send_sem=hop_send.at[d, st, p], recv_sem=hop_recv.at[d, st, p],
            device_id=second_axis(1 if d == 0 else n - 1), device_id_type=MESH,
        )
        return hops[p, d, st]

    second_later = (a + 1 < n, a == 0)
    for d in range(2):
        cp = hop(0, d, 1)

        @pl.when(jnp.logical_not(second_later[d]))
        def _(cp=cp):
            cp.start()

    row = lax.broadcasted_iota(jnp.int32, (2 * sel, sel), 0)
    col = lax.broadcasted_iota(jnp.int32, (2 * sel, sel), 1)
    even = (row == 2 * col).astype(F32)
    odd = (row == 2 * col + 1).astype(F32)
    spread_a = jnp.concatenate([even, odd], axis=1).astype(BF16)
    spread_b = jnp.concatenate([odd, -even], axis=1).astype(BF16)
    hots = [onehot_rows(listed_ref[k : k + 1, :], nv) for k in range(prods)]
    loads[0].wait()
    for k in range(prods):
        ops = sinkv[op_ref[k, 0]]
        g_re = jnp.dot(hots[k], ops[0], preferred_element_type=F32).astype(BF16)
        g_im = jnp.dot(hots[k], ops[1], preferred_element_type=F32).astype(BF16)
        g = jnp.concatenate([g_re, g_im], axis=0)
        left_a = jnp.dot(spread_a, g, preferred_element_type=F32).astype(BF16)
        left_b = jnp.dot(spread_b, g, preferred_element_type=F32).astype(BF16)
        lhs[:, k, :, 0:nv] = left_a.reshape(n_y, 2 * own, nv)
        lhs[:, k, :, nv : 2 * nv] = left_b.reshape(n_y, 2 * own, nv)

    exchange = []
    for s in range(NS):
        loads[1 + 2 * s].wait()
        loads[2 + 2 * s].wait()
        m = jnp.dot(
            lhs[...].reshape(n_y * prods * 2 * own, 2 * nv),
            perv[s].reshape(2 * nv, perv.shape[3]),
            preferred_element_type=F32,
        )
        sendb[s] = m.astype(BF16).reshape(sendb.shape[1:])
        recvb[s, y] = sendb[s, y]
        for i in range(1, n_y):
            if s == 0:
                await_answer(i - 1)
            cp = pltpu.make_async_remote_copy(
                src_ref=sendb.at[s, (y + i) % n_y], dst_ref=recvb.at[s, y],
                send_sem=a2a_send.at[s, i], recv_sem=a2a_recv.at[s, i],
                device_id=at_y(i), device_id_type=MESH,
            )
            cp.start()
            exchange.append(cp)

    for k in range(prods):
        pos = slot_ref[source_ref[0] * prods + op_ref[k, 1]]
        pt = pos // 16
        pc = pt % CORES
        px = (pt // CORES) % n
        pz = pt // (CORES * n)
        pa = (1 - pc) * pz + pc * px
        pb = (1 - pc) * px + pc * pz
        idx = ((pc * n + pa) * n + pb) * 16 + pos % 16
        for j in range(nv // 128):
            hot[pl.ds(k * nv + j * 128, 128), :] = onehot_rows(idx[j : j + 1, :], hot.shape[1])

    @pl.when(c == 1)
    def _():
        for i in range(1, n):

            @pl.when(b + i < n)
            def _(i=i):
                pl.semaphore_wait(ready_b.at[i], 1)
                phase1[i].start()

    def pass_on(p, d, st):
        part = tbl.at[c, (a + n - st) % n if d == 0 else (a + st) % n, (b + n - p) % n]
        cp = pltpu.make_async_remote_copy(
            src_ref=part, dst_ref=part,
            send_sem=fw_send.at[d, st, p], recv_sem=fw_recv.at[d, st, p],
            device_id=partner, device_id_type=MESH,
        )
        cp.start()
        forward[p, d, st] = cp

    def enter(p):
        if p > 0:
            phase1[p].wait_recv()
            hop(p, 0, 1).start()
            hop(p, 1, 1).start()
        else:
            for d in range(2):

                @pl.when(second_later[d])
                def _(d=d):
                    pl.semaphore_wait(ready_a.at[1 if d == 0 else n - 1], 1)
                    hops[0, d, 1].start()

            await_answer(len(peers) - 1)
        pass_on(p, 0, 0)

    def relay(p, st):
        for d in range(2):
            if (p, d, st) in hops:
                hops[p, d, st].wait_recv()
                if st + 1 < half or (st + 1 == half and d == p % 2):
                    hop(p, d, st + 1).start()
                pass_on(p, d, st)

    span = n * 16
    width = nv // 2

    def pick(st):
        for p in range(n):
            for d in range(2):
                if (p, d, st) in forward:
                    forward[p, d, st].wait_recv()
        blocks = []
        for core, at in ((c, a), (1 - c, b)):
            for i in (st, n - st) if 0 < st < half else (st,):
                blocks.append((core, (at + i) % n))
        pairs = [blocks[i : i + 2] for i in range(0, len(blocks), 2)]

        def column(j, carry):
            at = pl.ds(pl.multiple_of((j % 2) * width, width), width)
            got = None
            for pair in pairs:
                left = jnp.concatenate(
                    [
                        hot[:, pl.ds(pl.multiple_of((core * n + blk) * span, span), span)]
                        for core, blk in pair
                    ],
                    axis=1,
                )
                rows = jnp.concatenate(
                    [tbl[core, blk, :, j // 2, :, at].reshape(span, width) for core, blk in pair],
                    axis=0,
                )
                part = jnp.dot(left, rows, preferred_element_type=F32)
                got = part if got is None else got + part
            got = got.astype(BF16).reshape(prods, nv, width)
            to = pl.ds(pl.multiple_of(j * width, width), width)
            if st == 0:
                right[:, :, to] = got
            else:
                right[:, :, to] = right[:, :, to] + got
            return carry

        lax.fori_loop(0, 4, column, 0)

    arrival = [min(p, n - p) for p in range(n)]
    steps = []
    for p in range(n):
        start = 0.5 * (arrival[p] + 1) if p else 0.0
        steps.append((start, 0, p, enter, (p,)))
        for st in range(1, half + 1):
            steps.append((start + st, st, p, relay, (p, st)))
    for st in range(half + 1):
        steps.append((3.2 + st, half + 1, st, pick, (st,)))
    for _, _, _, act, args in sorted(steps, key=lambda step: step[:3]):
        act(*args)

    for cp in exchange:
        cp.wait_recv()
    per_t = n_y // NS
    group = NS // 2
    rows = group * NS * 2 * own
    parity = lax.broadcasted_iota(jnp.int32, (rows, nv), 0) % 2
    for k in range(prods):
        for m in range(2):
            got = recvb[m * group : (m + 1) * group].reshape(
                group * NS, per_t, prods * 2 * own, nv // per_t
            )
            mixed = jnp.concatenate(
                [
                    got[:, h, k * 2 * own : (k + 1) * 2 * own, :].reshape(rows, nv // per_t)
                    for h in range(per_t)
                ],
                axis=1,
            )
            both = jnp.dot(mixed, right[k], preferred_element_type=F32)
            by_re = both[:, :nv]
            by_im = both[:, nv:]
            turned = jnp.where(
                parity == 0, -pltpu.roll(by_im, rows - 1, 0), pltpu.roll(by_im, 1, 0)
            )
            res = (by_re + turned).astype(BF16).reshape(group, NS, 2 * own, nv)
            for tt in range(NS):
                out_ref[k, m * group : (m + 1) * group, :, tt * nv : (tt + 1) * nv] = res[:, tt]

    for cp in phase1[1:] + exchange + list(hops.values()) + list(forward.values()):
        cp.wait_send()


def per_device(peramb, sink_ops, op_table, row_slot, pair_source, op_index, listed_rows):
    n_y = lax.axis_size("col")
    nv = op_table.shape[2]
    cols = peramb.shape[3]
    prods, sel = listed_rows.shape
    own = sel // n_y
    shard = op_table.shape[0]
    order = NS * nv
    slots = lax.axis_size("tpair") * shard
    half = SIDE // 2
    dma = pltpu.SemaphoreType.DMA
    vmem = pl.BlockSpec(memory_space=pltpu.VMEM)
    smem = pl.BlockSpec(memory_space=pltpu.SMEM)
    hbm = pl.BlockSpec(memory_space=pl.ANY)
    out = pl.pallas_call(
        kernel,
        out_shape=pltpu.VMEM((prods, NS, 2 * own, order), BF16),
        in_specs=[smem, smem, vmem, vmem, hbm, hbm, vmem],
        out_specs=vmem,
        scratch_shapes=[
            pltpu.VMEM((NS, 2, nv, cols), BF16),
            pltpu.VMEM(sink_ops.shape[1:], BF16),
            pltpu.VMEM((n_y, prods, 2 * own, 2 * nv), BF16),
            pltpu.VMEM((NS, n_y, prods * 2 * own, cols), BF16),
            pltpu.VMEM((NS, n_y, prods * 2 * own, cols), BF16),
            pltpu.VMEM((CORES, SIDE, SIDE, 2, shard, nv), BF16),
            pltpu.VMEM((prods * nv, slots), BF16),
            pltpu.VMEM((prods, nv, 2 * nv), BF16),
            dma((1 + 2 * NS,)),
            dma((NS, n_y)),
            dma((NS, n_y)),
            dma((SIDE,)),
            dma((SIDE,)),
            dma((2, half + 1, SIDE)),
            dma((2, half + 1, SIDE)),
            dma((2, half + 1, SIDE)),
            dma((2, half + 1, SIDE)),
            pltpu.SemaphoreType.REGULAR((n_y,)),
            pltpu.SemaphoreType.REGULAR((SIDE,)),
            pltpu.SemaphoreType.REGULAR((SIDE,)),
            pltpu.SemaphoreType.REGULAR((1,)),
        ],
        compiler_params=pltpu.CompilerParams(
            collective_id=0, has_side_effects=True, vmem_limit_bytes=56 << 20
        ),
        name="contract",
    )(
        pair_source,
        op_index,
        listed_rows,
        row_slot.reshape(-1, nv // 128, 128),
        peramb,
        sink_ops,
        op_table,
    )
    return out.reshape(prods, NS, own, 2, order)


def solution(mesh):
    in_specs = (
        P("tpair", None, None, "col"),
        P("tpair", None, None, None, None),
        P("tpair", None, None),
        P(),
        P("tpair"),
        P("tpair", None),
        P("tpair", None),
    )
    out_specs = P("tpair", None, "col", None, None)
    return jax.shard_map(
        per_device, mesh=mesh, in_specs=in_specs, out_specs=out_specs, check_vma=False
    )
```

```python
import jax
import jax.numpy as jnp
from jax import lax
from jax.experimental import pallas as pl
from jax.experimental.pallas import tpu as pltpu
from jax.sharding import PartitionSpec as P

NS = 4
CORES = 2
SIDE = 8
MESH = pl.DeviceIdType.MESH
BF16 = jnp.bfloat16
F32 = jnp.float32


def column_of(row):
    n = row.shape[1]
    return jnp.transpose(jnp.broadcast_to(row, (n, n)))


def onehot_rows(row, width, base=0):
    col = column_of(row)
    n = col.shape[0]
    lane = lax.broadcasted_iota(jnp.int32, (n, n), 1) + base
    parts = [(col == lane + w * n).astype(F32).astype(BF16) for w in range(width // n)]
    return jnp.concatenate(parts, axis=1)


def kernel(
    source_ref, op_ref, listed_hbm, slot_hbm, peramb_ref, sink_ref, optab_hbm, out_ref,
    listed_ref, slot_ref, optab_ref, perv, sinkv, lhs, sendb, recvb, tbl, hot, right,
    in_sem, a2a_send, a2a_recv, p1_send, p1_recv, hop_send, hop_recv, fw_send, fw_recv,
    ready_y, ready_b, ready_a, ready_c,
):
    nv = sinkv.shape[3]
    n_y = sendb.shape[1]
    own = sendb.shape[2] // (2 * CORES)
    prods = op_ref.shape[0]
    sel = listed_hbm.shape[1]
    n = SIDE
    half = n // 2
    t = lax.axis_index("tpair")
    y = lax.axis_index("col")
    c = t % CORES
    x = (t // CORES) % n
    z = t // (CORES * n)

    a = (1 - c) * z + c * x
    b = (1 - c) * x + c * z

    def ring_id(a_, b_):
        z_ = (1 - c) * a_ + c * b_
        x_ = (1 - c) * b_ + c * a_
        return ((z_ * n + x_) * CORES + c, y)

    def first_axis(i):
        return ring_id(a, (b + i) % n)

    def second_axis(i):
        return ring_id((a + i) % n, b)

    def at_y(i):
        return (t, (y + i) % n_y)

    partner = (t + 1 - 2 * c, y)

    loads = [pltpu.make_async_copy(sink_ref.at[0], sinkv, in_sem.at[0])]
    for s in range(NS):
        for r in range(2):
            loads.append(
                pltpu.make_async_copy(
                    peramb_ref.at[0, r, pl.ds(s * nv, nv)], perv.at[s, r], in_sem.at[1 + s * 2 + r]
                )
            )
    small = [
        pltpu.make_async_copy(src, dst, in_sem.at[len(loads) + i])
        for i, (src, dst) in enumerate(
            ((optab_hbm, optab_ref), (listed_hbm, listed_ref), (slot_hbm, slot_ref))
        )
    ]
    for cp in small + loads:
        cp.start()

    peers = []
    for i in range(1, n_y):
        peers.append((at_y(i), y + i < n_y, ready_y.at[i], ready_y.at[n_y - i]))
    for i in range(1, n):
        peers.append((first_axis(i), b + i < n, ready_b.at[i], ready_b.at[n - i]))
    for i in (1, n - 1):
        peers.append((second_axis(i), a + i < n, ready_a.at[i], ready_a.at[n - i]))
    peers.append((partner, c == 1, ready_c.at[0], ready_c.at[0]))
    barrier = pltpu.get_barrier_semaphore()
    for dev, later, _, _ in peers:

        @pl.when(later)
        def _(dev=dev):
            pl.semaphore_signal(barrier, inc=1, device_id=dev, device_id_type=MESH)

    small[0].wait()
    shard = optab_ref[...].astype(F32)
    for r in range(2):
        tbl[c, a, b, r] = shard[:, r, :].astype(BF16)

    earlier = y + b + (a + n - 1) // n + (a + 1) // n + 1 - c

    @pl.when(earlier > 0)
    def _():
        pl.semaphore_wait(barrier, earlier)

    for dev, later, _, theirs in peers:

        @pl.when(jnp.logical_not(later))
        def _(dev=dev, theirs=theirs):
            pl.semaphore_signal(theirs, inc=1, device_id=dev, device_id_type=MESH)

    def await_answer(index):
        _, later, mine, _ = peers[index]

        @pl.when(later)
        def _():
            pl.semaphore_wait(mine, 1)

    def shard_copy(i):
        return pltpu.make_async_remote_copy(
            src_ref=tbl.at[c, a, b], dst_ref=tbl.at[c, a, b],
            send_sem=p1_send.at[i], recv_sem=p1_recv.at[i],
            device_id=first_axis(i), device_id_type=MESH,
        )

    phase1 = [None] + [shard_copy(i) for i in range(1, n)]
    far_first = sorted(range(1, n), key=lambda i: -min(i, n - i))
    for i in far_first:

        @pl.when(b + i >= n)
        def _(i=i):
            phase1[i].start()

    @pl.when(c == 0)
    def _():
        for i in far_first:

            @pl.when(b + i < n)
            def _(i=i):
                pl.semaphore_wait(ready_b.at[i], 1)
                phase1[i].start()

    row = lax.broadcasted_iota(jnp.int32, (2 * sel, sel), 0)
    col = lax.broadcasted_iota(jnp.int32, (2 * sel, sel), 1)
    even = (row == 2 * col).astype(F32)
    odd = (row == 2 * col + 1).astype(F32)
    spread_a = jnp.concatenate([even, odd], axis=1).astype(BF16)
    spread_b = jnp.concatenate([odd, -even], axis=1).astype(BF16)
    small[1].wait()
    hots = [onehot_rows(listed_ref[k : k + 1, :], nv) for k in range(prods)]
    loads[0].wait()
    for k in range(prods):
        ops = sinkv[op_ref[k, 0]]
        g_re = jnp.dot(hots[k], ops[0], preferred_element_type=F32).astype(BF16)
        g_im = jnp.dot(hots[k], ops[1], preferred_element_type=F32).astype(BF16)
        g = jnp.concatenate([g_re, g_im], axis=0)
        left_a = jnp.dot(spread_a, g, preferred_element_type=F32).astype(BF16)
        left_b = jnp.dot(spread_b, g, preferred_element_type=F32).astype(BF16)
        lhs[:, k, :, 0:nv] = left_a.reshape(n_y, 2 * own, nv)
        lhs[:, k, :, nv : 2 * nv] = left_b.reshape(n_y, 2 * own, nv)

    exchange = []
    for s in range(NS):
        loads[1 + 2 * s].wait()
        loads[2 + 2 * s].wait()
        m = jnp.dot(
            lhs[...].reshape(n_y * prods * 2 * own, 2 * nv),
            perv[s].reshape(2 * nv, perv.shape[3]),
            preferred_element_type=F32,
        )
        sendb[s] = m.astype(BF16).reshape(sendb.shape[1:])
        recvb[s, y] = sendb[s, y]
        for i in range(1, n_y):
            if s == 0:
                await_answer(i - 1)
            cp = pltpu.make_async_remote_copy(
                src_ref=sendb.at[s, (y + i) % n_y], dst_ref=recvb.at[s, y],
                send_sem=a2a_send.at[s, i], recv_sem=a2a_recv.at[s, i],
                device_id=at_y(i), device_id_type=MESH,
            )
            cp.start()
            exchange.append(cp)

    @pl.when(c == 1)
    def _():
        for i in range(1, n):

            @pl.when(b + i < n)
            def _(i=i):
                pl.semaphore_wait(ready_b.at[i], 1)
                phase1[i].start()

    small[2].wait()
    for k in range(prods):
        pos = slot_ref[source_ref[0] * prods + op_ref[k, 1]]
        pt = pos // 16
        pc = pt % CORES
        px = (pt // CORES) % n
        pz = pt // (CORES * n)
        pa = (1 - pc) * pz + pc * px
        pb = (1 - pc) * px + pc * pz
        idx = ((pc * n + pa) * n + pb) * 16 + pos % 16
        for j in range(nv // 128):
            hot[pl.ds(k * nv + j * 128, 128), :] = onehot_rows(idx[j : j + 1, :], hot.shape[1])

    for cp in phase1[1:]:
        cp.wait_recv()

    hops = {}
    forward = {}

    def hop(d, st, h):
        part = tbl.at[c, (a + n - st + 1) % n if d == 0 else (a + st - 1) % n, pl.ds(h * half, half)]
        cp = pltpu.make_async_remote_copy(
            src_ref=part, dst_ref=part,
            send_sem=hop_send.at[d, st, h], recv_sem=hop_recv.at[d, st, h],
            device_id=second_axis(1 if d == 0 else n - 1), device_id_type=MESH,
        )
        cp.start()
        hops[d, st, h] = cp
        if st == half:
            near, col_y = second_axis(1 if d == 0 else n - 1)
            cp = pltpu.make_async_remote_copy(
                src_ref=part, dst_ref=part,
                send_sem=fw_send.at[d, st, h], recv_sem=fw_recv.at[d, st, h],
                device_id=(near + 1 - 2 * c, col_y), device_id_type=MESH,
            )
            cp.start()
            forward[d, st, h] = cp

    def pass_on(d, st, h):
        part = tbl.at[c, (a + n - st) % n if d == 0 else (a + st) % n, pl.ds(h * half, half)]
        cp = pltpu.make_async_remote_copy(
            src_ref=part, dst_ref=part,
            send_sem=fw_send.at[d, st, h], recv_sem=fw_recv.at[d, st, h],
            device_id=partner, device_id_type=MESH,
        )
        cp.start()
        forward[d, st, h] = cp

    def relay(st):
        for h in range(2):
            for d in range(2):
                if (d, st, h) in hops:
                    hops[d, st, h].wait_recv()
                    if st + 1 < half or (st + 1 == half and h == d):
                        hop(d, st + 1, h)
                    if st < half:
                        pass_on(d, st, h)

    span = n * 16
    width = nv // 2

    def pick(st):
        for d in range(2):
            for h in range(2):
                if (d, st, h) in forward:
                    forward[d, st, h].wait_recv()
        blocks = []
        for core, at in ((c, a), (1 - c, b)):
            for i in (st, n - st) if 0 < st < half else (st,):
                blocks.append((core, (at + i) % n))
        pairs = [blocks[i : i + 2] for i in range(0, len(blocks), 2)]

        def column(j, carry):
            at = pl.ds(pl.multiple_of((j % 2) * width, width), width)
            got = None
            for pair in pairs:
                left = jnp.concatenate(
                    [
                        hot[:, pl.ds(pl.multiple_of((core * n + blk) * span, span), span)]
                        for core, blk in pair
                    ],
                    axis=1,
                )
                rows = jnp.concatenate(
                    [tbl[core, blk, :, j // 2, :, at].reshape(span, width) for core, blk in pair],
                    axis=0,
                )
                part = jnp.dot(left, rows, preferred_element_type=F32)
                got = part if got is None else got + part
            got = got.astype(BF16).reshape(prods, nv, width)
            to = pl.ds(pl.multiple_of(j * width, width), width)
            if st == 0:
                right[:, :, to] = got
            else:
                right[:, :, to] = right[:, :, to] + got
            return carry

        lax.fori_loop(0, 4, column, 0)

    await_answer(n_y - 1 + n - 1)
    for h in range(2):
        hop(0, 1, h)
    await_answer(n_y - 1 + n + 1)
    for h in range(2):
        pass_on(0, 0, h)
    await_answer(n_y - 1 + n)
    for h in range(2):
        hop(1, 1, h)
    relay(1)
    pick(0)
    relay(2)
    pick(1)
    relay(3)
    pick(2)
    relay(4)
    pick(3)
    pick(4)

    for cp in exchange:
        cp.wait_recv()
    per_t = n_y // NS
    group = NS // 2
    rows = group * NS * 2 * own
    parity = lax.broadcasted_iota(jnp.int32, (rows, nv), 0) % 2
    for k in range(prods):
        for m in range(2):
            got = recvb[m * group : (m + 1) * group].reshape(
                group * NS, per_t, prods * 2 * own, nv // per_t
            )
            mixed = jnp.concatenate(
                [
                    got[:, h, k * 2 * own : (k + 1) * 2 * own, :].reshape(rows, nv // per_t)
                    for h in range(per_t)
                ],
                axis=1,
            )
            both = jnp.dot(mixed, right[k], preferred_element_type=F32)
            by_re = both[:, :nv]
            by_im = both[:, nv:]
            turned = jnp.where(
                parity == 0, -pltpu.roll(by_im, rows - 1, 0), pltpu.roll(by_im, 1, 0)
            )
            res = (by_re + turned).astype(BF16).reshape(group, NS, 2 * own, nv)
            for tt in range(NS):
                out_ref[k, m * group : (m + 1) * group, :, tt * nv : (tt + 1) * nv] = res[:, tt]

    for cp in phase1[1:] + exchange + list(hops.values()) + list(forward.values()):
        cp.wait_send()


def per_device(peramb, sink_ops, op_table, row_slot, pair_source, op_index, listed_rows):
    n_y = lax.axis_size("col")
    nv = op_table.shape[2]
    cols = peramb.shape[3]
    prods, sel = listed_rows.shape
    own = sel // n_y
    shard = op_table.shape[0]
    order = NS * nv
    slots = lax.axis_size("tpair") * shard
    half = SIDE // 2
    dma = pltpu.SemaphoreType.DMA
    vmem = pl.BlockSpec(memory_space=pltpu.VMEM)
    smem = pl.BlockSpec(memory_space=pltpu.SMEM)
    hbm = pl.BlockSpec(memory_space=pl.ANY)
    out = pl.pallas_call(
        kernel,
        out_shape=pltpu.VMEM((prods, NS, 2 * own, order), BF16),
        in_specs=[smem, smem, hbm, hbm, hbm, hbm, hbm],
        out_specs=vmem,
        scratch_shapes=[
            pltpu.VMEM(listed_rows.shape, jnp.int32),
            pltpu.VMEM((row_slot.shape[0] // nv, nv // 128, 128), jnp.int32),
            pltpu.VMEM(op_table.shape, BF16),
            pltpu.VMEM((NS, 2, nv, cols), BF16),
            pltpu.VMEM(sink_ops.shape[1:], BF16),
            pltpu.VMEM((n_y, prods, 2 * own, 2 * nv), BF16),
            pltpu.VMEM((NS, n_y, prods * 2 * own, cols), BF16),
            pltpu.VMEM((NS, n_y, prods * 2 * own, cols), BF16),
            pltpu.VMEM((CORES, SIDE, SIDE, 2, shard, nv), BF16),
            pltpu.VMEM((prods * nv, slots), BF16),
            pltpu.VMEM((prods, nv, 2 * nv), BF16),
            dma((4 + 2 * NS,)),
            dma((NS, n_y)),
            dma((NS, n_y)),
            dma((SIDE,)),
            dma((SIDE,)),
            dma((2, half + 1, 2)),
            dma((2, half + 1, 2)),
            dma((2, half + 1, 2)),
            dma((2, half + 1, 2)),
            pltpu.SemaphoreType.REGULAR((n_y,)),
            pltpu.SemaphoreType.REGULAR((SIDE,)),
            pltpu.SemaphoreType.REGULAR((SIDE,)),
            pltpu.SemaphoreType.REGULAR((1,)),
        ],
        compiler_params=pltpu.CompilerParams(
            collective_id=0, has_side_effects=True, vmem_limit_bytes=56 << 20
        ),
        name="contract",
    )(
        pair_source,
        op_index,
        listed_rows,
        row_slot.reshape(-1, nv // 128, 128),
        peramb,
        sink_ops,
        op_table,
    )
    return out.reshape(prods, NS, own, 2, order)


def solution(mesh):
    in_specs = (
        P("tpair", None, None, "col"),
        P("tpair", None, None, None, None),
        P("tpair", None, None),
        P(),
        P("tpair"),
        P("tpair", None),
        P("tpair", None),
    )
    out_specs = P("tpair", None, "col", None, None)
    return jax.shard_map(
        per_device, mesh=mesh, in_specs=in_specs, out_specs=out_specs, check_vma=False
    )
```

```python
import jax
import jax.numpy as jnp
from jax import lax
from jax.experimental import pallas as pl
from jax.experimental.pallas import tpu as pltpu
from jax.sharding import PartitionSpec as P

NS = 4
CORES = 2
SIDE = 8
MESH = pl.DeviceIdType.MESH
BF16 = jnp.bfloat16
F32 = jnp.float32


def column_of(row):
    n = row.shape[1]
    return jnp.transpose(jnp.broadcast_to(row, (n, n)))


def onehot_rows(row, width, base=0):
    col = column_of(row)
    n = col.shape[0]
    lane = lax.broadcasted_iota(jnp.int32, (n, n), 1) + base
    parts = [(col == lane + w * n).astype(F32).astype(BF16) for w in range(width // n)]
    return jnp.concatenate(parts, axis=1)


def kernel(
    source_ref, op_ref, listed_hbm, slot_hbm, peramb_ref, sink_ref, optab_hbm, out_ref,
    listed_ref, slot_ref, optab_ref, perv, sinkv, lhs, sendb, recvb, tbl, hot, right,
    in_sem, a2a_send, a2a_recv, p1_send, p1_recv, hop_send, hop_recv, fw_send, fw_recv,
    ready_y, ready_b, ready_a, ready_c,
):
    nv = sinkv.shape[3]
    n_y = sendb.shape[1]
    own = sendb.shape[2] // (2 * CORES)
    prods = op_ref.shape[0]
    sel = listed_hbm.shape[1]
    n = SIDE
    half = n // 2
    t = lax.axis_index("tpair")
    y = lax.axis_index("col")
    c = t % CORES
    x = (t // CORES) % n
    z = t // (CORES * n)

    a = (1 - c) * z + c * x
    b = (1 - c) * x + c * z

    def ring_id(a_, b_):
        z_ = (1 - c) * a_ + c * b_
        x_ = (1 - c) * b_ + c * a_
        return ((z_ * n + x_) * CORES + c, y)

    def first_axis(i):
        return ring_id(a, (b + i) % n)

    def second_axis(i):
        return ring_id((a + i) % n, b)

    def at_y(i):
        return (t, (y + i) % n_y)

    partner = (t + 1 - 2 * c, y)

    loads = [pltpu.make_async_copy(sink_ref.at[0], sinkv, in_sem.at[0])]
    for s in range(NS):
        for r in range(2):
            loads.append(
                pltpu.make_async_copy(
                    peramb_ref.at[0, r, pl.ds(s * nv, nv)], perv.at[s, r], in_sem.at[1 + s * 2 + r]
                )
            )
    small = [
        pltpu.make_async_copy(src, dst, in_sem.at[len(loads) + i])
        for i, (src, dst) in enumerate(
            ((optab_hbm, optab_ref), (listed_hbm, listed_ref), (slot_hbm, slot_ref))
        )
    ]
    for cp in small + loads:
        cp.start()

    peers = []
    for i in range(1, n_y):
        peers.append((at_y(i), y + i < n_y, ready_y.at[i], ready_y.at[n_y - i]))
    for i in range(1, n):
        peers.append((first_axis(i), b + i < n, ready_b.at[i], ready_b.at[n - i]))
    for i in (1, n - 1):
        peers.append((second_axis(i), a + i < n, ready_a.at[i], ready_a.at[n - i]))
    peers.append((partner, c == 1, ready_c.at[0], ready_c.at[0]))
    barrier = pltpu.get_barrier_semaphore()
    for dev, later, _, _ in peers:

        @pl.when(later)
        def _(dev=dev):
            pl.semaphore_signal(barrier, inc=1, device_id=dev, device_id_type=MESH)

    small[0].wait()
    shard = optab_ref[...].astype(F32)
    for r in range(2):
        tbl[c, a, b, r] = shard[:, r, :].astype(BF16)

    earlier = y + b + (a + n - 1) // n + (a + 1) // n + 1 - c

    @pl.when(earlier > 0)
    def _():
        pl.semaphore_wait(barrier, earlier)

    for dev, later, _, theirs in peers:

        @pl.when(jnp.logical_not(later))
        def _(dev=dev, theirs=theirs):
            pl.semaphore_signal(theirs, inc=1, device_id=dev, device_id_type=MESH)

    def await_answer(index):
        _, later, mine, _ = peers[index]

        @pl.when(later)
        def _():
            pl.semaphore_wait(mine, 1)

    def shard_copy(i):
        return pltpu.make_async_remote_copy(
            src_ref=tbl.at[c, a, b], dst_ref=tbl.at[c, a, b],
            send_sem=p1_send.at[i], recv_sem=p1_recv.at[i],
            device_id=first_axis(i), device_id_type=MESH,
        )

    phase1 = [None] + [shard_copy(i) for i in range(1, n)]
    far_first = sorted(range(1, n), key=lambda i: -min(i, n - i))
    for i in far_first:

        @pl.when(b + i >= n)
        def _(i=i):
            phase1[i].start()

    @pl.when(c == 0)
    def _():
        for i in far_first:

            @pl.when(b + i < n)
            def _(i=i):
                pl.semaphore_wait(ready_b.at[i], 1)
                phase1[i].start()

    row = lax.broadcasted_iota(jnp.int32, (2 * sel, sel), 0)
    col = lax.broadcasted_iota(jnp.int32, (2 * sel, sel), 1)
    even = (row == 2 * col).astype(F32)
    odd = (row == 2 * col + 1).astype(F32)
    spread_a = jnp.concatenate([even, odd], axis=1).astype(BF16)
    spread_b = jnp.concatenate([odd, -even], axis=1).astype(BF16)
    small[1].wait()
    hots = [onehot_rows(listed_ref[k : k + 1, :], nv) for k in range(prods)]
    loads[0].wait()
    for k in range(prods):
        ops = sinkv[op_ref[k, 0]]
        g_re = jnp.dot(hots[k], ops[0], preferred_element_type=F32).astype(BF16)
        g_im = jnp.dot(hots[k], ops[1], preferred_element_type=F32).astype(BF16)
        g = jnp.concatenate([g_re, g_im], axis=0)
        left_a = jnp.dot(spread_a, g, preferred_element_type=F32).astype(BF16)
        left_b = jnp.dot(spread_b, g, preferred_element_type=F32).astype(BF16)
        lhs[:, k, :, 0:nv] = left_a.reshape(n_y, 2 * own, nv)
        lhs[:, k, :, nv : 2 * nv] = left_b.reshape(n_y, 2 * own, nv)

    exchange = []
    for s in range(NS):
        loads[1 + 2 * s].wait()
        loads[2 + 2 * s].wait()
        m = jnp.dot(
            lhs[...].reshape(n_y * prods * 2 * own, 2 * nv),
            perv[s].reshape(2 * nv, perv.shape[3]),
            preferred_element_type=F32,
        )
        sendb[s] = m.astype(BF16).reshape(sendb.shape[1:])
        recvb[s, y] = sendb[s, y]
        for i in range(1, n_y):
            if s == 0:
                await_answer(i - 1)
            cp = pltpu.make_async_remote_copy(
                src_ref=sendb.at[s, (y + i) % n_y], dst_ref=recvb.at[s, y],
                send_sem=a2a_send.at[s, i], recv_sem=a2a_recv.at[s, i],
                device_id=at_y(i), device_id_type=MESH,
            )
            cp.start()
            exchange.append(cp)

    @pl.when(c == 1)
    def _():
        for i in range(1, n):

            @pl.when(b + i < n)
            def _(i=i):
                pl.semaphore_wait(ready_b.at[i], 1)
                phase1[i].start()

    small[2].wait()
    for k in range(prods):
        pos = slot_ref[source_ref[0] * prods + op_ref[k, 1]]
        pt = pos // 16
        pc = pt % CORES
        px = (pt // CORES) % n
        pz = pt // (CORES * n)
        pa = (1 - pc) * pz + pc * px
        pb = (1 - pc) * px + pc * pz
        idx = ((pc * n + pa) * n + pb) * 16 + pos % 16
        for j in range(nv // 128):
            hot[pl.ds(k * nv + j * 128, 128), :] = onehot_rows(idx[j : j + 1, :], hot.shape[1])

    for cp in phase1[1:]:
        cp.wait_recv()

    hops = {}
    forward = {}

    def hop(d, st, h):
        part = tbl.at[c, (a + n - st + 1) % n if d == 0 else (a + st - 1) % n, pl.ds(h * half, half)]
        cp = pltpu.make_async_remote_copy(
            src_ref=part, dst_ref=part,
            send_sem=hop_send.at[d, st, h], recv_sem=hop_recv.at[d, st, h],
            device_id=second_axis(1 if d == 0 else n - 1), device_id_type=MESH,
        )
        cp.start()
        hops[d, st, h] = cp
        if st == half:
            near, col_y = second_axis(1 if d == 0 else n - 1)
            cp = pltpu.make_async_remote_copy(
                src_ref=part, dst_ref=part,
                send_sem=fw_send.at[d, st, h], recv_sem=fw_recv.at[d, st, h],
                device_id=(near + 1 - 2 * c, col_y), device_id_type=MESH,
            )
            cp.start()
            forward[d, st, h] = cp

    def pass_on(d, st, h):
        part = tbl.at[c, (a + n - st) % n if d == 0 else (a + st) % n, pl.ds(h * half, half)]
        cp = pltpu.make_async_remote_copy(
            src_ref=part, dst_ref=part,
            send_sem=fw_send.at[d, st, h], recv_sem=fw_recv.at[d, st, h],
            device_id=partner, device_id_type=MESH,
        )
        cp.start()
        forward[d, st, h] = cp

    def relay(st):
        for h in range(2):
            for d in range(2):
                if (d, st, h) in hops:
                    hops[d, st, h].wait_recv()
                    if st + 1 < half or (st + 1 == half and h == d):
                        hop(d, st + 1, h)
                    if st < half:
                        pass_on(d, st, h)

    span = n * 16
    width = nv

    def pick(st):
        for d in range(2):
            for h in range(2):
                if (d, st, h) in forward:
                    forward[d, st, h].wait_recv()
        blocks = []
        for core, at in ((c, a), (1 - c, b)):
            for i in (st, n - st) if 0 < st < half else (st,):
                blocks.append((core, (at + i) % n))
        pairs = [blocks[i : i + 2] for i in range(0, len(blocks), 2)]

        def column(j, carry):
            got = None
            for pair in pairs:
                left = jnp.concatenate(
                    [
                        hot[:, pl.ds(pl.multiple_of((core * n + blk) * span, span), span)]
                        for core, blk in pair
                    ],
                    axis=1,
                )
                rows = jnp.concatenate(
                    [tbl[core, blk, :, j].reshape(span, width) for core, blk in pair],
                    axis=0,
                )
                part = jnp.dot(left, rows, preferred_element_type=F32)
                got = part if got is None else got + part
            got = got.astype(BF16).reshape(prods, nv, width)
            to = pl.ds(pl.multiple_of(j * width, width), width)
            if st == 0:
                right[:, :, to] = got
            else:
                right[:, :, to] = right[:, :, to] + got
            return carry

        lax.fori_loop(0, 2, column, 0)

    await_answer(n_y - 1 + n - 1)
    for h in range(2):
        hop(0, 1, h)
    await_answer(n_y - 1 + n + 1)
    for h in range(2):
        pass_on(0, 0, h)
    await_answer(n_y - 1 + n)
    for h in range(2):
        hop(1, 1, h)
    relay(1)
    pick(0)
    relay(2)
    pick(1)
    relay(3)
    pick(2)
    pick(3)
    relay(4)
    pick(4)

    for cp in exchange:
        cp.wait_recv()
    per_t = n_y // NS
    group = NS // 2
    rows = group * NS * 2 * own
    parity = lax.broadcasted_iota(jnp.int32, (rows, nv), 0) % 2
    for k in range(prods):
        for m in range(2):
            got = recvb[m * group : (m + 1) * group].reshape(
                group * NS, per_t, prods * 2 * own, nv // per_t
            )
            mixed = jnp.concatenate(
                [
                    got[:, h, k * 2 * own : (k + 1) * 2 * own, :].reshape(rows, nv // per_t)
                    for h in range(per_t)
                ],
                axis=1,
            )
            both = jnp.dot(mixed, right[k], preferred_element_type=F32)
            by_re = both[:, :nv]
            by_im = both[:, nv:]
            turned = jnp.where(
                parity == 0, -pltpu.roll(by_im, rows - 1, 0), pltpu.roll(by_im, 1, 0)
            )
            res = (by_re + turned).astype(BF16).reshape(group, NS, 2 * own, nv)
            for tt in range(NS):
                out_ref[k, m * group : (m + 1) * group, :, tt * nv : (tt + 1) * nv] = res[:, tt]

    for cp in phase1[1:] + exchange + list(hops.values()) + list(forward.values()):
        cp.wait_send()


def per_device(peramb, sink_ops, op_table, row_slot, pair_source, op_index, listed_rows):
    n_y = lax.axis_size("col")
    nv = op_table.shape[2]
    cols = peramb.shape[3]
    prods, sel = listed_rows.shape
    own = sel // n_y
    shard = op_table.shape[0]
    order = NS * nv
    slots = lax.axis_size("tpair") * shard
    half = SIDE // 2
    dma = pltpu.SemaphoreType.DMA
    vmem = pl.BlockSpec(memory_space=pltpu.VMEM)
    smem = pl.BlockSpec(memory_space=pltpu.SMEM)
    hbm = pl.BlockSpec(memory_space=pl.ANY)
    out = pl.pallas_call(
        kernel,
        out_shape=pltpu.VMEM((prods, NS, 2 * own, order), BF16),
        in_specs=[smem, smem, hbm, hbm, hbm, hbm, hbm],
        out_specs=vmem,
        scratch_shapes=[
            pltpu.VMEM(listed_rows.shape, jnp.int32),
            pltpu.VMEM((row_slot.shape[0] // nv, nv // 128, 128), jnp.int32),
            pltpu.VMEM(op_table.shape, BF16),
            pltpu.VMEM((NS, 2, nv, cols), BF16),
            pltpu.VMEM(sink_ops.shape[1:], BF16),
            pltpu.VMEM((n_y, prods, 2 * own, 2 * nv), BF16),
            pltpu.VMEM((NS, n_y, prods * 2 * own, cols), BF16),
            pltpu.VMEM((NS, n_y, prods * 2 * own, cols), BF16),
            pltpu.VMEM((CORES, SIDE, SIDE, 2, shard, nv), BF16),
            pltpu.VMEM((prods * nv, slots), BF16),
            pltpu.VMEM((prods, nv, 2 * nv), BF16),
            dma((4 + 2 * NS,)),
            dma((NS, n_y)),
            dma((NS, n_y)),
            dma((SIDE,)),
            dma((SIDE,)),
            dma((2, half + 1, 2)),
            dma((2, half + 1, 2)),
            dma((2, half + 1, 2)),
            dma((2, half + 1, 2)),
            pltpu.SemaphoreType.REGULAR((n_y,)),
            pltpu.SemaphoreType.REGULAR((SIDE,)),
            pltpu.SemaphoreType.REGULAR((SIDE,)),
            pltpu.SemaphoreType.REGULAR((1,)),
        ],
        compiler_params=pltpu.CompilerParams(
            collective_id=0, has_side_effects=True, vmem_limit_bytes=56 << 20
        ),
        name="contract",
    )(
        pair_source,
        op_index,
        listed_rows,
        row_slot.reshape(-1, nv // 128, 128),
        peramb,
        sink_ops,
        op_table,
    )
    return out.reshape(prods, NS, own, 2, order)


def solution(mesh):
    in_specs = (
        P("tpair", None, None, "col"),
        P("tpair", None, None, None, None),
        P("tpair", None, None),
        P(),
        P("tpair"),
        P("tpair", None),
        P("tpair", None),
    )
    out_specs = P("tpair", None, "col", None, None)
    return jax.shard_map(
        per_device, mesh=mesh, in_specs=in_specs, out_specs=out_specs, check_vma=False
    )
```
